128 devices in a mesh: occ: 8 (over z_hi, y), virt: 4 (over z_lo, core), aux: 4 (over x).
Axes of the slice: x: 4, y: 4, z: 4 (z_hi: 2, z_lo: 2; z = z_hi * 2 + z_lo), core: 2. Of those that a mesh axis runs over, the one named last changes fastest.
Arguments:
- factors: bfloat16 [3072, 16, 1024], P('aux', 'occ', 'virt'), may hold values from -2 to 2
- occ_energy: float32 [16], replicated, may hold values from -2 to -0.3
- virt_energy: float32 [1024], replicated, may hold values from 0.2 to 3
Outputs:
- density: float32 [3072, 16, 1024], P('aux', 'occ', 'virt')
The draws below stay inside these ranges and needn't reach their ends.
All inputs are finite; a program needn't handle non-finite values.
Results may differ from the reference program's by a relative error of at most 0.0016.
Values may be sent and summed in bfloat16 or wider, within the bound.
No kernel may reach another device: no remote copies, remote signals or barrier semaphores. Data moves between devices by JAX's collectives and lax.ppermute only.
A program may use at most 128 MiB of HBM per device.

```python
import jax
import jax.numpy as jnp
from jax import lax

NAUX = 3072
NVIRT = 1024
OCC_DEV = 2
NOCC = 16
STEPS = 3


def steps_of(rng, shape, shards, smallest, top_value):
    level = 1.0
    for axis_at, blocks in shards:
        steps = jax.random.uniform(jax.random.fold_in(jax.random.fold_in(rng, 6), axis_at), (blocks,), jnp.float32, smallest / len(shards), top_value / len(shards))
        level = level * jnp.repeat(jnp.exp(steps), shape[axis_at] // blocks).reshape((-1,) + (1,) * (len(shape) - 1 - axis_at))
    return level


def normal_values(key, dims, scale, limit, cuts=(), kind=jnp.bfloat16):
    drawn = jax.random.normal(key, dims, jnp.float32) * scale
    if len(cuts) > 0:
        drawn = steps_of(key, dims, cuts, -0.22, 0.18) * drawn
    return jnp.clip(drawn, min=-limit, max=limit).astype(kind)


def setup_inputs(seed: int = 0) -> dict:
    streams_of = jax.random.split(jax.random.key(seed), 4)
    return {
        "factors": normal_values(streams_of[0], (NAUX, NOCC, NVIRT), (NAUX ** -0.25), 2.0, ((0, 4), (1, 8), (2, 4))),
        "occ_energy": jnp.clip(jax.random.uniform(streams_of[1], (NOCC,), jnp.float32, -2.0, -0.3), -2.0, -0.3),
        "virt_energy": jnp.clip(jax.random.uniform(streams_of[2], (NVIRT,), jnp.float32, 0.2, 3.0), 0.2, 3.0),
    }


def reference(factors, occ_energy, virt_energy):
    blocks = NOCC // OCC_DEV
    whole = factors.astype(jnp.float32).reshape(NAUX, blocks, OCC_DEV, NVIRT)
    energy_blocks = occ_energy.reshape(blocks, OCC_DEV)
    density = jnp.zeros((blocks, NAUX, OCC_DEV, NVIRT), jnp.float32)

    def one_block(items):
        local, partner, eo_i, eo_j = items
        ints = jnp.einsum('qia,qjb->iajb', local, partner, precision=lax.Precision.HIGHEST)
        gap = eo_i[:, None, None, None] + eo_j[None, None, :, None] - virt_energy[None, :, None, None] - virt_energy[None, None, None, :]
        amps = lax.optimization_barrier((ints / gap).astype(jnp.bfloat16)).astype(jnp.float32)
        return jnp.einsum('iajb,qjb->qia', amps, partner, precision=lax.Precision.HIGHEST)

    local_all = jnp.moveaxis(whole, 1, 0)
    for step in range(STEPS):
        partner_all = jnp.roll(local_all, step, axis=0)
        partner_energy = jnp.roll(energy_blocks, step, axis=0)
        density = density + lax.map(one_block, (local_all, partner_all, energy_blocks, partner_energy))
    return jnp.moveaxis(density, 0, 1).reshape(NAUX, NOCC, NVIRT)
```

```python
import jax
import jax.numpy as jnp
from jax import lax
from jax.sharding import PartitionSpec as P


AXES = ("occ", "virt", "aux")
HIGH, LONG, LOW, CORES, RING = 2, 4, 2, 2, 4


def moves(place):
    pairs = []
    for z_hi in range(HIGH):
        for y in range(LONG):
            for z_lo in range(LOW):
                for core in range(CORES):
                    for x in range(RING):
                        ends = []
                        for h, w, l, c, r in ((z_hi, y, z_lo, core, x), place(z_hi, y, z_lo, core, x)):
                            ends.append((((h * LONG + w) * LOW + l) * CORES + c) * RING + r)
                        pairs.append(tuple(ends))
    return pairs


def chain_step(z_hi, y, z_lo, core, x):
    if y < LONG - 1:
        return z_hi, y + 1, z_lo, core, x
    return 1 - z_hi, 0, 1 - z_lo, core, x


NEXT = moves(chain_step)
PAIR = moves(lambda h, y, l, c, x: (h, y, 1 - l, c, x))
CORE = moves(lambda h, y, l, c, x: (h, y, l, 1 - c, x))
ALONG = [moves(lambda h, y, l, c, x, k=k: (h, y, l, c, (x + k) % RING)) for k in range(RING)]


def send(value, pairs):
    return lax.ppermute(value, AXES, pairs)


def on_device(factors, occ_energy, virt_energy):
    rows = factors.shape[0]
    part = lax.axis_index("occ")
    virt = lax.axis_index("virt")
    x = lax.axis_index("aux")
    y = part % LONG
    z_lo = virt // CORES
    core = virt % CORES

    quarters = jnp.stack([factors[:, q // 2, 128 * (q % 2) : 128 * (q % 2) + 128] for q in range(4)])
    turned = lax.dynamic_slice_in_dim(jnp.concatenate([quarters, quarters[:3]]), x, 4, axis=0)

    first = [turned[0]] + [send(turned[k], ALONG[k]) for k in (1, 2, 3)]
    own = jnp.stack(first)
    rest = [jnp.concatenate([turned[1], turned[2], turned[3]], axis=1)]
    for k in (1, 2, 3):
        rest.append(send(jnp.concatenate([turned[(k + j) % 4] for j in (1, 2, 3)], axis=1), ALONG[k]))

    y1 = send(own, NEXT)
    z0 = send(own, PAIR)
    own_c = send(own, CORE)
    y2 = send(y1, NEXT)
    z1 = send(y1, PAIR)
    y1_c = send(y1, CORE)
    z0_c = send(z0, CORE)
    z2 = send(y2[:2], PAIR)
    y3 = send(z1[2:], NEXT)
    y2_c = send(y2, CORE)
    z1_c = send(z1, CORE)
    last = jnp.concatenate([z2, y3])
    last_c = send(last, CORE)

    local = jnp.concatenate([jnp.concatenate([first[k], rest[k]], axis=1) for k in range(4)], axis=0)

    sets = [
        (z_lo, (own, own_c, z0, z0_c)),
        (z_lo ^ (y < 1).astype(z_lo.dtype), (y1, y1_c, z1, z1_c)),
        (z_lo ^ (y < 2).astype(z_lo.dtype), (y2, y2_c, last, last_c)),
    ]

    quarter_of = [(x + r) % 4 for r in range(4)]
    eo_i = jnp.concatenate(
        [jnp.broadcast_to(lax.dynamic_slice_in_dim(occ_energy, 2 * part + q // 2, 1), (128,)) for q in quarter_of]
    )
    ev_a = jnp.concatenate(
        [lax.dynamic_slice_in_dim(virt_energy, 256 * virt + 128 * (q % 2), 128) for q in quarter_of]
    )

    total = None
    for s, (low, pieces) in enumerate(sets):
        wide = jnp.concatenate([piece.reshape(4 * rows, 128) for piece in pieces], axis=1)
        ints = lax.dot_general(local, wide, (((0,), (0,)), ((), ())), preferred_element_type=jnp.float32)
        eo_j = lax.dynamic_slice_in_dim(occ_energy, 2 * jnp.mod(part - s + 8, 8) + x // 2, 1)
        ev_b = jnp.concatenate(
            [
                lax.dynamic_slice_in_dim(virt_energy, 256 * (2 * l + c) + 128 * (x % 2), 128)
                for l in (low, 1 - low)
                for c in (core, 1 - core)
            ]
        )
        gap = (eo_i + eo_j - ev_a)[:, None] - ev_b[None, :]
        amps = (ints / gap).astype(jnp.bfloat16)
        given = lax.dot_general(wide, amps, (((1,), (1,)), ((), ())), preferred_element_type=jnp.float32)
        total = given if total is None else total + given

    out = total[:rows]
    columns = [out[:, 128 * r : 128 * r + 128] for r in range(4)]
    for k in (1, 2, 3):
        got = send(total[k * rows : (k + 1) * rows].astype(jnp.bfloat16), ALONG[4 - k])
        for r in range(4):
            q = (r - k) % 4
            columns[r] = columns[r] + got[:, 128 * q : 128 * q + 128].astype(jnp.float32)
    back = jnp.stack(columns)
    back = lax.dynamic_slice_in_dim(jnp.concatenate([back, back[:3]]), jnp.mod(4 - x, 4), 4, axis=0)
    return back.reshape(2, 2, rows, 128).transpose(2, 0, 1, 3).reshape(rows, 2, 256)


def solution(mesh):
    return jax.shard_map(
        on_device,
        mesh=mesh,
        in_specs=(P("aux", "occ", "virt"), P(), P()),
        out_specs=P("aux", "occ", "virt"),
        check_vma=False,
    )
```

```python
import functools

import jax
import jax.numpy as jnp
from jax import lax
from jax.experimental import pallas as pl
from jax.experimental.pallas import tpu as pltpu
from jax.sharding import PartitionSpec as P


AXES = ("occ", "virt", "aux")
HIGH, LONG, LOW, CORES, RING = 2, 4, 2, 2, 4
BLOCKS = HIGH * LONG
ROWS, TILE = 768, 128
F32, BF16 = jnp.float32, jnp.bfloat16
LIMIT = 6 << 20


def moves(place):
    pairs = []
    for z_hi in range(HIGH):
        for y in range(LONG):
            for z_lo in range(LOW):
                for core in range(CORES):
                    for x in range(RING):
                        ends = []
                        for h, w, l, c, r in ((z_hi, y, z_lo, core, x), place(z_hi, y, z_lo, core, x)):
                            ends.append((((h * LONG + w) * LOW + l) * CORES + c) * RING + r)
                        pairs.append(tuple(ends))
    return pairs


def chain_step(z_hi, y, z_lo, core, x):
    if y < LONG - 1:
        return z_hi, y + 1, z_lo, core, x
    return 1 - z_hi, 0, 1 - z_lo, core, x


NEXT = moves(chain_step)
NEXT2 = moves(lambda *place: chain_step(*chain_step(*place)))
PAIR = moves(lambda h, y, l, c, x: (h, y, 1 - l, c, x))
CORE = moves(lambda h, y, l, c, x: (h, y, l, 1 - c, x))
ALONG = [moves(lambda h, y, l, c, x, k=k: (h, y, l, c, (x + k) % RING)) for k in range(RING)]


def send(value, pairs):
    return lax.ppermute(value, AXES, pairs)


class Gathered:
    def __init__(self):
        self.arrays = []

    def block(self, array, index):
        for at, known in enumerate(self.arrays):
            if known is array:
                return at, index
        self.arrays.append(array)
        return len(self.arrays) - 1, index

    def piece(self, blocks):
        return [self.block(*block) for block in blocks]


def amplitudes_body(step, labels, local, pieces, *refs):
    occ_ref, lane_ref, out_ref = refs[-3:]
    load = lambda block: refs[block[0]][block[1]]
    part = lax.axis_index("occ")
    virt = lax.axis_index("virt")
    x = lax.axis_index("aux")
    y = lax.rem(part, LONG)
    core = lax.rem(virt, CORES)
    low = lax.rem(lax.div(virt, CORES) + jnp.where(y < step, 1, 0), LOW)
    half = lax.rem(x, 2)
    eo_j = occ_ref[2 * lax.rem(part - step + BLOCKS, BLOCKS) + lax.div(x, 2)]
    lanes = []
    for r in range(RING):
        q = lax.rem(x + r, RING)
        eo_i = occ_ref[2 * part + lax.div(q, 2)]
        lanes.append((eo_i + eo_j) - lane_ref[pl.ds(2 * virt + lax.rem(q, 2), 1), :])
    lane = jnp.concatenate(lanes, axis=1)
    for n in range(0, len(labels), 2):
        total = None
        for k in range(RING):
            wide = jnp.concatenate([load(pieces[n][k]), load(pieces[n + 1][k])], axis=1)
            mine = jnp.concatenate([load(local[r][k]) for r in range(RING)], axis=1)
            given = lax.dot_general(wide, mine, (((0,), (0,)), ((), ())), preferred_element_type=F32)
            total = given if total is None else total + given
        for m in (0, 1):
            other_low, other_core = labels[n + m]
            l = lax.rem(low + other_low, LOW)
            c = lax.rem(core + other_core, CORES)
            ev_b = lane_ref[pl.ds(2 * (CORES * l + c) + half, 1), :]
            column = jnp.transpose(jnp.broadcast_to(ev_b, (TILE, TILE)))
            gap = lane - jnp.concatenate([column] * RING, axis=1)
            ints = total[TILE * m : TILE * m + TILE, :]
            out_ref[TILE * (n + m) : TILE * (n + m) + TILE, :] = (ints / gap).astype(BF16)


VMEM = pl.BlockSpec(memory_space=pltpu.VMEM)


def here(values):
    return [pltpu.with_memory_space_constraint(value, pltpu.VMEM) for value in values]


def amplitudes(step, labels, local, pieces, energies):
    gathered = Gathered()
    local = [gathered.piece(blocks) for blocks in local]
    pieces = [gathered.piece(blocks) for blocks in pieces]
    return pl.pallas_call(
        functools.partial(amplitudes_body, step, labels, local, pieces),
        out_shape=pltpu.VMEM((TILE * len(labels), RING * TILE), BF16),
        in_specs=[VMEM] * len(gathered.arrays) + [pl.BlockSpec(memory_space=pltpu.SMEM), VMEM],
        out_specs=VMEM,
        compiler_params=pltpu.CompilerParams(vmem_limit_bytes=LIMIT),
    )(*here(gathered.arrays), *energies)


def density_body(groups, before, chunk, *refs):
    out_ref = refs[-1]
    deep = 256

    def step(k, rows):
        total = None
        for pieces, amps in groups:
            wide = jnp.concatenate([refs[piece[k][0]][piece[k][1], rows, :] for piece in pieces], axis=1)
            given = jnp.dot(wide, refs[amps][...], preferred_element_type=F32)
            total = given if total is None else total + given
        if before is not None:
            total = total + refs[before][k, rows, :]
        return total.astype(out_ref.dtype)

    for i in range(ROWS // deep):
        rows = slice(deep * i, deep * i + deep)
        if chunk is None:
            for k in range(RING):
                out_ref[k, rows, :] = step(k, rows)
        else:
            out_ref[rows, :] = step(chunk, rows)


def density(groups, before, chunk, kind):
    gathered = Gathered()
    places = []
    for pieces, amps in groups:
        if chunk is not None:
            pieces = [[piece[chunk]] * RING for piece in pieces]
        places.append(([gathered.piece(piece) for piece in pieces], gathered.block(amps, 0)[0]))
    held = None if before is None else gathered.block(before, 0)[0]
    shape = (RING, ROWS, RING * TILE) if chunk is None else (ROWS, RING * TILE)
    return pl.pallas_call(
        functools.partial(density_body, places, held, chunk),
        out_shape=pltpu.VMEM(shape, kind),
        in_specs=[VMEM] * len(gathered.arrays),
        out_specs=VMEM,
        compiler_params=pltpu.CompilerParams(vmem_limit_bytes=LIMIT),
    )(*here(gathered.arrays))


def finish_body(own_ref, *refs):
    got, out_ref = refs[:-1], refs[-1]
    x = lax.axis_index("aux")
    columns = []
    for r in range(RING):
        total = own_ref[:, TILE * r : TILE * r + TILE]
        for k in (1, 2, 3):
            q = (r - k) % RING
            total = total + got[k - 1][:, TILE * q : TILE * q + TILE].astype(F32)
        columns.append(total)
    for v in range(RING):

        @pl.when(x == v)
        def _():
            for q in range(RING):
                i, start = q // 2, TILE * (q % 2)
                out_ref[:, i, start : start + TILE] = columns[(q - v) % RING]


def finish(own, got):
    return pl.pallas_call(
        finish_body,
        out_shape=jax.ShapeDtypeStruct((ROWS, 2, 2 * TILE), F32),
        in_specs=[VMEM] * 4,
        out_specs=VMEM,
        name="finish",
        compiler_params=pltpu.CompilerParams(vmem_limit_bytes=LIMIT),
    )(*here([own, *got]))


def steps(factors, occ_energy, virt_energy):
    x = lax.axis_index("aux")
    energies = (occ_energy, virt_energy.reshape(8, TILE))

    quarters = jnp.stack([factors[:, q // 2, TILE * (q % 2) : TILE * (q % 2) + TILE] for q in range(RING)])
    turned = lax.dynamic_slice_in_dim(jnp.concatenate([quarters, quarters[:3]]), x, RING, axis=0)

    turned = lax.optimization_barrier(turned)
    came = {k: send(turned[k], ALONG[k]) for k in (1, 2, 3)}
    rest = {}
    for k in (1, 2, 3):
        rest[k] = send(jnp.stack([turned[(k + j) % RING] for j in (1, 2, 3)]), ALONG[k])
    own = (jnp.stack([turned[0], came[1]]), jnp.stack([came[2], came[3]]))

    both = (0, 1)
    y1 = [send(own[h], NEXT) for h in both]
    z0 = [send(own[h], PAIR) for h in both]
    y2 = [send(y1[h], NEXT) for h in both]
    z1 = [send(y1[h], PAIR) for h in both]
    z2 = send(y2[0], PAIR)
    y3 = send(z0[1], NEXT2)
    swap = lambda pair: [send(pair[h], CORE) for h in both]
    own_c = swap(own)
    z0_c = swap(z0)
    y1_c = swap(y1)
    z1_c = swap(z1)
    y2_c = swap(y2)
    last_c = swap((z2, y3))

    halves = lambda low, high: [(low, 0), (low, 1), (high, 0), (high, 1)]
    local = [halves(*own)]
    for r in (1, 2, 3):
        local.append([(turned, r)] + [(rest[k], r - 1) for k in (1, 2, 3)])

    same = [(0, 0), (0, 1)]
    cross = [(1, 0), (1, 1)]
    set0 = [halves(*own), halves(*own_c), halves(*z0), halves(*z0_c)]
    set1 = [halves(*y1), halves(*y1_c), halves(*z1), halves(*z1_c)]
    set2 = [halves(*y2), halves(*y2_c)]
    set3 = [halves(z2, y3), halves(*last_c)]
    amps0 = amplitudes(0, same + cross, local, set0, energies)
    amps1 = amplitudes(1, same + cross, local, set1, energies)
    early = density([(set0, amps0)], None, None, F32)
    early = density([(set1, amps1)], early, None, F32)
    amps2 = amplitudes(2, same, local, set2, energies)
    amps3 = amplitudes(2, cross, local, set3, energies)
    late = [(set2, amps2), (set3, amps3)]
    got = {}
    for k in (2, 1, 3):
        part = density(late, early, k, BF16)
        got[k] = send(part, ALONG[RING - k])
    mine = density(late, early, 0, F32)
    return finish(mine, [got[k] for k in (1, 2, 3)])


def solution(mesh):
    return jax.shard_map(
        steps,
        mesh=mesh,
        in_specs=(P("aux", "occ", "virt"), P(), P()),
        out_specs=P("aux", "occ", "virt"),
        check_vma=False,
    )
```

```python
import functools

import jax
import jax.numpy as jnp
from jax import lax
from jax.experimental import pallas as pl
from jax.experimental.pallas import tpu as pltpu
from jax.sharding import PartitionSpec as P


AXES = ("occ", "virt", "aux")
HIGH, LONG, LOW, CORES, RING = 2, 4, 2, 2, 4
BLOCKS = HIGH * LONG
ROWS, TILE = 768, 128
F32, BF16 = jnp.float32, jnp.bfloat16
LIMIT = 6 << 20


def moves(place):
    pairs = []
    for z_hi in range(HIGH):
        for y in range(LONG):
            for z_lo in range(LOW):
                for core in range(CORES):
                    for x in range(RING):
                        ends = []
                        for h, w, l, c, r in ((z_hi, y, z_lo, core, x), place(z_hi, y, z_lo, core, x)):
                            ends.append((((h * LONG + w) * LOW + l) * CORES + c) * RING + r)
                        pairs.append(tuple(ends))
    return pairs


def chain_step(z_hi, y, z_lo, core, x):
    if y < LONG - 1:
        return z_hi, y + 1, z_lo, core, x
    return 1 - z_hi, 0, 1 - z_lo, core, x


def back_step(z_hi, y, z_lo, core, x):
    if y == 2:
        return 1 - z_hi, 1, 1 - z_lo, core, x
    return z_hi, (y - 1) % LONG, z_lo, core, x


NEXT = moves(chain_step)
PREV = moves(back_step)
PAIR = moves(lambda h, y, l, c, x: (h, y, 1 - l, c, x))
CORE = moves(lambda h, y, l, c, x: (h, y, l, 1 - c, x))
ALONG = [moves(lambda h, y, l, c, x, k=k: (h, y, l, c, (x + k) % RING)) for k in range(RING)]


def send(value, pairs):
    return lax.ppermute(value, AXES, pairs)


class Gathered:
    def __init__(self):
        self.arrays = []

    def block(self, array, index):
        for at, known in enumerate(self.arrays):
            if known is array:
                return at, index
        self.arrays.append(array)
        return len(self.arrays) - 1, index

    def piece(self, blocks):
        return [self.block(*block) for block in blocks]


def amplitudes_body(step, labels, local, pieces, *refs):
    occ_ref, lane_ref, out_ref = refs[-3:]
    load = lambda block: refs[block[0]][block[1]]
    part = lax.axis_index("occ")
    virt = lax.axis_index("virt")
    x = lax.axis_index("aux")
    y = lax.rem(part, LONG)
    core = lax.rem(virt, CORES)
    low = lax.rem(lax.div(virt, CORES) + jnp.where(y < step, 1, 0), LOW)
    half = lax.rem(x, 2)
    eo_j = occ_ref[2 * lax.rem(part - step + BLOCKS, BLOCKS) + lax.div(x, 2)]
    lanes = []
    for r in range(RING):
        q = lax.rem(x + r, RING)
        eo_i = occ_ref[2 * part + lax.div(q, 2)]
        lanes.append((eo_i + eo_j) - lane_ref[pl.ds(2 * virt + lax.rem(q, 2), 1), :])
    lane = jnp.concatenate(lanes, axis=1)
    for n in range(0, len(labels), 2):
        total = None
        for k in range(RING):
            wide = jnp.concatenate([load(pieces[n][k]), load(pieces[n + 1][k])], axis=1)
            mine = jnp.concatenate([load(local[r][k]) for r in range(RING)], axis=1)
            given = lax.dot_general(wide, mine, (((0,), (0,)), ((), ())), preferred_element_type=F32)
            total = given if total is None else total + given
        for m in (0, 1):
            other_low, other_core = labels[n + m]
            l = lax.rem(low + other_low, LOW)
            c = lax.rem(core + other_core, CORES)
            ev_b = lane_ref[pl.ds(2 * (CORES * l + c) + half, 1), :]
            column = jnp.transpose(jnp.broadcast_to(ev_b, (TILE, TILE)))
            gap = lane - jnp.concatenate([column] * RING, axis=1)
            ints = total[TILE * m : TILE * m + TILE, :]
            out_ref[TILE * (n + m) : TILE * (n + m) + TILE, :] = (ints / gap).astype(BF16)


VMEM = pl.BlockSpec(memory_space=pltpu.VMEM)


def here(values):
    return [pltpu.with_memory_space_constraint(value, pltpu.VMEM) for value in values]


def amplitudes(step, labels, local, pieces, energies):
    gathered = Gathered()
    local = [gathered.piece(blocks) for blocks in local]
    pieces = [gathered.piece(blocks) for blocks in pieces]
    return pl.pallas_call(
        functools.partial(amplitudes_body, step, labels, local, pieces),
        out_shape=pltpu.VMEM((TILE * len(labels), RING * TILE), BF16),
        in_specs=[VMEM] * len(gathered.arrays) + [pl.BlockSpec(memory_space=pltpu.SMEM), VMEM],
        out_specs=VMEM,
        compiler_params=pltpu.CompilerParams(vmem_limit_bytes=LIMIT),
    )(*here(gathered.arrays), *energies)


def density_body(groups, before, chunk, *refs):
    out_ref = refs[-1]
    deep = 256

    def step(k, rows):
        total = None
        for pieces, amps in groups:
            wide = jnp.concatenate([refs[piece[k][0]][piece[k][1], rows, :] for piece in pieces], axis=1)
            given = jnp.dot(wide, refs[amps][...], preferred_element_type=F32)
            total = given if total is None else total + given
        if before is not None:
            total = total + refs[before][k, rows, :]
        return total.astype(out_ref.dtype)

    for i in range(ROWS // deep):
        rows = slice(deep * i, deep * i + deep)
        if chunk is None:
            for k in range(RING):
                out_ref[k, rows, :] = step(k, rows)
        else:
            out_ref[rows, :] = step(chunk, rows)


def density(groups, before, chunk, kind):
    gathered = Gathered()
    places = []
    for pieces, amps in groups:
        if chunk is not None:
            pieces = [[piece[chunk]] * RING for piece in pieces]
        places.append(([gathered.piece(piece) for piece in pieces], gathered.block(amps, 0)[0]))
    held = None if before is None else gathered.block(before, 0)[0]
    shape = (RING, ROWS, RING * TILE) if chunk is None else (ROWS, RING * TILE)
    return pl.pallas_call(
        functools.partial(density_body, places, held, chunk),
        out_shape=pltpu.VMEM(shape, kind),
        in_specs=[VMEM] * len(gathered.arrays),
        out_specs=VMEM,
        compiler_params=pltpu.CompilerParams(vmem_limit_bytes=LIMIT),
    )(*here(gathered.arrays))


def finish_body(own_ref, *refs):
    got, out_ref = refs[:-1], refs[-1]
    x = lax.axis_index("aux")
    columns = []
    for r in range(RING):
        total = own_ref[:, TILE * r : TILE * r + TILE]
        for k in (1, 2, 3):
            q = (r - k) % RING
            total = total + got[k - 1][:, TILE * q : TILE * q + TILE].astype(F32)
        columns.append(total)
    for v in range(RING):

        @pl.when(x == v)
        def _():
            for q in range(RING):
                i, start = q // 2, TILE * (q % 2)
                out_ref[:, i, start : start + TILE] = columns[(q - v) % RING]


def finish(own, got):
    return pl.pallas_call(
        finish_body,
        out_shape=jax.ShapeDtypeStruct((ROWS, 2, 2 * TILE), F32),
        in_specs=[VMEM] * 4,
        out_specs=VMEM,
        name="finish",
        compiler_params=pltpu.CompilerParams(vmem_limit_bytes=LIMIT),
    )(*here([own, *got]))


def steps(factors, occ_energy, virt_energy):
    x = lax.axis_index("aux")
    energies = (occ_energy, virt_energy.reshape(8, TILE))

    quarters = jnp.stack([factors[:, q // 2, TILE * (q % 2) : TILE * (q % 2) + TILE] for q in range(RING)])
    turned = lax.dynamic_slice_in_dim(jnp.concatenate([quarters, quarters[:3]]), x, RING, axis=0)

    turned = lax.optimization_barrier(turned)
    came = {k: send(turned[k], ALONG[k]) for k in (1, 2, 3)}
    rest = {}
    for k in (1, 2, 3):
        rest[k] = send(jnp.stack([turned[(k + j) % RING] for j in (1, 2, 3)]), ALONG[k])
    own = (jnp.stack([turned[0], came[1]]), jnp.stack([came[2], came[3]]))

    both = (0, 1)
    y1 = [send(own[h], NEXT) for h in both]
    z0 = [send(own[h], PAIR) for h in both]
    m1 = [send(own[h], PREV) for h in both]
    m2 = [send(m1[h], PREV) for h in both]
    u1 = send(z0[0], NEXT)
    z1 = send(y1[1], PAIR)
    z2 = send(m2[0], PAIR)
    u2 = send(z1, NEXT)
    swap = lambda pair: [send(pair[h], CORE) for h in both]
    own_c = swap(own)
    z0_c = swap(z0)
    y1_c = swap(y1)
    far_c = swap((u1, z1))
    m2_c = swap(m2)
    last_c = swap((z2, u2))

    halves = lambda low, high: [(low, 0), (low, 1), (high, 0), (high, 1)]
    local = [halves(*own)]
    for r in (1, 2, 3):
        local.append([(turned, r)] + [(rest[k], r - 1) for k in (1, 2, 3)])

    same = [(0, 0), (0, 1)]
    cross = [(1, 0), (1, 1)]
    set0 = [halves(*own), halves(*own_c), halves(*z0), halves(*z0_c)]
    set1 = [halves(*y1), halves(*y1_c), halves(u1, z1), halves(*far_c)]
    set2 = [halves(*m2), halves(*m2_c)]
    set3 = [halves(z2, u2), halves(*last_c)]
    amps0 = amplitudes(0, same + cross, local, set0, energies)
    amps1 = amplitudes(1, same + cross, local, set1, energies)
    amps2 = amplitudes(2, same, local, set2, energies)
    amps3 = amplitudes(2, cross, local, set3, energies)
    all_sets = [(set0, amps0), (set1, amps1), (set2, amps2), (set3, amps3)]
    got = {}
    for k in (2, 1, 3):
        part = density(all_sets, None, k, BF16)
        got[k] = send(part, ALONG[RING - k])
    mine = density(all_sets, None, 0, F32)
    return finish(mine, [got[k] for k in (1, 2, 3)])


def solution(mesh):
    return jax.shard_map(
        steps,
        mesh=mesh,
        in_specs=(P("aux", "occ", "virt"), P(), P()),
        out_specs=P("aux", "occ", "virt"),
        check_vma=False,
    )
```

```python
import functools

import jax
import jax.numpy as jnp
from jax import lax
from jax.experimental import pallas as pl
from jax.experimental.pallas import tpu as pltpu
from jax.sharding import PartitionSpec as P


AXES = ("occ", "virt", "aux")
HIGH, LONG, LOW, CORES, RING = 2, 4, 2, 2, 4
BLOCKS = HIGH * LONG
ROWS, TILE = 768, 128
F32, BF16 = jnp.float32, jnp.bfloat16
LIMIT = 6 << 20


def moves(place):
    pairs = []
    for z_hi in range(HIGH):
        for y in range(LONG):
            for z_lo in range(LOW):
                for core in range(CORES):
                    for x in range(RING):
                        ends = []
                        for h, w, l, c, r in ((z_hi, y, z_lo, core, x), place(z_hi, y, z_lo, core, x)):
                            ends.append((((h * LONG + w) * LOW + l) * CORES + c) * RING + r)
                        pairs.append(tuple(ends))
    return pairs


def chain_step(z_hi, y, z_lo, core, x):
    if y < LONG - 1:
        return z_hi, y + 1, z_lo, core, x
    return 1 - z_hi, 0, 1 - z_lo, core, x


def back_step(z_hi, y, z_lo, core, x):
    if y == 2:
        return 1 - z_hi, 1, 1 - z_lo, core, x
    return z_hi, (y - 1) % LONG, z_lo, core, x


NEXT = moves(chain_step)
PREV = moves(back_step)
PAIR = moves(lambda h, y, l, c, x: (h, y, 1 - l, c, x))
CORE = moves(lambda h, y, l, c, x: (h, y, l, 1 - c, x))
ALONG = [moves(lambda h, y, l, c, x, k=k: (h, y, l, c, (x + k) % RING)) for k in range(RING)]


def send(value, pairs):
    return lax.ppermute(value, AXES, pairs)


def prepare_body(factors_ref, turned_ref, *refs):
    firsts, rests, wide = refs[:3], refs[3:6], refs[6]
    x = lax.axis_index("aux")
    wide[...] = factors_ref[...].astype(F32)
    for q in range(RING):
        value = wide[pl.ds(2 * (q % 2) + q // 2, ROWS, stride=RING), :].astype(BF16)
        t = lax.rem(q - x + RING, RING)
        turned_ref[t] = value
        for k in (1, 2, 3):

            @pl.when(t == k)
            def _():
                firsts[k - 1][...] = value

            @pl.when(t != k)
            def _():
                rests[k - 1][lax.rem(t - k - 1 + 2 * RING, RING)] = value


def prepare(factors):
    rows = factors.reshape(ROWS, 2, 2, TILE).transpose(0, 2, 1, 3).reshape(RING * ROWS, TILE)
    return pl.pallas_call(
        prepare_body,
        out_shape=[pltpu.VMEM((RING, ROWS, TILE), BF16)]
        + [pltpu.VMEM((ROWS, TILE), BF16)] * 3
        + [pltpu.VMEM((3, ROWS, TILE), BF16)] * 3,
        in_specs=[VMEM],
        out_specs=[VMEM] * 7,
        scratch_shapes=[pltpu.VMEM((RING * ROWS, TILE), F32)],
        name="prepare",
        compiler_params=pltpu.CompilerParams(vmem_limit_bytes=LIMIT),
    )(rows)


class Gathered:
    def __init__(self):
        self.arrays = []

    def block(self, array, index):
        for at, known in enumerate(self.arrays):
            if known is array:
                return at, index
        self.arrays.append(array)
        return len(self.arrays) - 1, index

    def piece(self, blocks):
        return [self.block(*block) for block in blocks]


def amplitudes_body(step, labels, local, pieces, *refs):
    occ_ref, lane_ref, out_ref = refs[-3:]
    load = lambda block: refs[block[0]][block[1]]
    part = lax.axis_index("occ")
    virt = lax.axis_index("virt")
    x = lax.axis_index("aux")
    y = lax.rem(part, LONG)
    core = lax.rem(virt, CORES)
    low = lax.rem(lax.div(virt, CORES) + jnp.where(y < step, 1, 0), LOW)
    half = lax.rem(x, 2)
    eo_j = occ_ref[2 * lax.rem(part - step + BLOCKS, BLOCKS) + lax.div(x, 2)]
    lanes = []
    for r in range(RING):
        q = lax.rem(x + r, RING)
        eo_i = occ_ref[2 * part + lax.div(q, 2)]
        lanes.append((eo_i + eo_j) - lane_ref[pl.ds(2 * virt + lax.rem(q, 2), 1), :])
    lane = jnp.concatenate(lanes, axis=1)
    for n in range(0, len(labels), 2):
        total = None
        for k in range(RING):
            wide = jnp.concatenate([load(pieces[n][k]), load(pieces[n + 1][k])], axis=1)
            mine = jnp.concatenate([load(local[r][k]) for r in range(RING)], axis=1)
            given = lax.dot_general(wide, mine, (((0,), (0,)), ((), ())), preferred_element_type=F32)
            total = given if total is None else total + given
        for m in (0, 1):
            other_low, other_core = labels[n + m]
            l = lax.rem(low + other_low, LOW)
            c = lax.rem(core + other_core, CORES)
            ev_b = lane_ref[pl.ds(2 * (CORES * l + c) + half, 1), :]
            column = jnp.transpose(jnp.broadcast_to(ev_b, (TILE, TILE)))
            gap = lane - jnp.concatenate([column] * RING, axis=1)
            ints = total[TILE * m : TILE * m + TILE, :]
            out_ref[TILE * (n + m) : TILE * (n + m) + TILE, :] = (ints / gap).astype(BF16)


VMEM = pl.BlockSpec(memory_space=pltpu.VMEM)


def here(values):
    return [pltpu.with_memory_space_constraint(value, pltpu.VMEM) for value in values]


def amplitudes(step, labels, local, pieces, energies):
    gathered = Gathered()
    local = [gathered.piece(blocks) for blocks in local]
    pieces = [gathered.piece(blocks) for blocks in pieces]
    return pl.pallas_call(
        functools.partial(amplitudes_body, step, labels, local, pieces),
        out_shape=pltpu.VMEM((TILE * len(labels), RING * TILE), BF16),
        in_specs=[VMEM] * len(gathered.arrays) + [pl.BlockSpec(memory_space=pltpu.SMEM), VMEM],
        out_specs=VMEM,
        compiler_params=pltpu.CompilerParams(vmem_limit_bytes=LIMIT),
    )(*here(gathered.arrays), *energies)


def density_body(groups, before, chunk, *refs):
    out_ref = refs[-1]
    deep = 256

    def step(k, rows):
        total = None
        for pieces, amps in groups:
            wide = jnp.concatenate([refs[piece[k][0]][piece[k][1], rows, :] for piece in pieces], axis=1)
            given = jnp.dot(wide, refs[amps][...], preferred_element_type=F32)
            total = given if total is None else total + given
        if before is not None:
            total = total + (refs[before][k, rows, :] if chunk is None else refs[before][rows, :])
        return total.astype(out_ref.dtype)

    for i in range(ROWS // deep):
        rows = slice(deep * i, deep * i + deep)
        if chunk is None:
            for k in range(RING):
                out_ref[k, rows, :] = step(k, rows)
        else:
            out_ref[rows, :] = step(chunk, rows)


def density(groups, before, chunk, kind):
    gathered = Gathered()
    places = []
    for pieces, amps in groups:
        if chunk is not None:
            pieces = [[piece[chunk]] * RING for piece in pieces]
        places.append(([gathered.piece(piece) for piece in pieces], gathered.block(amps, 0)[0]))
    held = None if before is None else gathered.block(before, 0)[0]
    shape = (RING, ROWS, RING * TILE) if chunk is None else (ROWS, RING * TILE)
    return pl.pallas_call(
        functools.partial(density_body, places, held, chunk),
        out_shape=pltpu.VMEM(shape, kind),
        in_specs=[VMEM] * len(gathered.arrays),
        out_specs=VMEM,
        compiler_params=pltpu.CompilerParams(vmem_limit_bytes=LIMIT),
    )(*here(gathered.arrays))


def finish_body(own_ref, *refs):
    got, out_ref = refs[:-1], refs[-1]
    x = lax.axis_index("aux")
    columns = []
    for r in range(RING):
        total = own_ref[:, TILE * r : TILE * r + TILE]
        for k in (1, 2, 3):
            q = (r - k) % RING
            total = total + got[k - 1][:, TILE * q : TILE * q + TILE].astype(F32)
        columns.append(total)
    for v in range(RING):

        @pl.when(x == v)
        def _():
            for q in range(RING):
                at = 2 * (q % 2) + q // 2
                out_ref[pl.ds(at, ROWS, stride=RING), :] = columns[(q - v) % RING]


def finish(own, got):
    return pl.pallas_call(
        finish_body,
        out_shape=jax.ShapeDtypeStruct((RING * ROWS, TILE), F32),
        in_specs=[VMEM] * 4,
        out_specs=VMEM,
        name="finish",
        compiler_params=pltpu.CompilerParams(vmem_limit_bytes=LIMIT),
    )(*here([own, *got]))


def steps(factors, occ_energy, virt_energy):
    energies = (occ_energy, virt_energy.reshape(8, TILE))

    turned, *ready = prepare(factors)
    came = {k: send(ready[k - 1], ALONG[k]) for k in (1, 2, 3)}
    rest = {k: send(ready[k + 2], ALONG[k]) for k in (1, 2, 3)}
    own = (jnp.stack([turned[0], came[1]]), jnp.stack([came[2], came[3]]))

    both = (0, 1)
    y1 = [send(own[h], NEXT) for h in both]
    z0 = [send(own[h], PAIR) for h in both]
    m1 = [send(own[h], PREV) for h in both]
    m2 = [send(m1[h], PREV) for h in both]
    u1 = send(z0[0], NEXT)
    z1 = send(y1[1], PAIR)
    z2 = send(m2[0], PAIR)
    u2 = send(z1, NEXT)
    swap = lambda pair: [send(pair[h], CORE) for h in both]
    own_c = swap(own)
    z0_c = swap(z0)
    y1_c = swap(y1)
    far_c = swap((u1, z1))
    m2_c = swap(m2)
    last_c = swap((z2, u2))

    halves = lambda low, high: [(low, 0), (low, 1), (high, 0), (high, 1)]
    local = [halves(*own)]
    for r in (1, 2, 3):
        local.append([(turned, r)] + [(rest[k], r - 1) for k in (1, 2, 3)])

    same = [(0, 0), (0, 1)]
    cross = [(1, 0), (1, 1)]
    set0 = [halves(*own), halves(*own_c), halves(*z0), halves(*z0_c)]
    set1 = [halves(*y1), halves(*y1_c), halves(u1, z1), halves(*far_c)]
    set2 = [halves(*m2), halves(*m2_c)]
    set3 = [halves(z2, u2), halves(*last_c)]
    amps0 = amplitudes(0, same + cross, local, set0, energies)
    amps1 = amplitudes(1, same + cross, local, set1, energies)
    amps2 = amplitudes(2, same, local, set2, energies)
    amps3 = amplitudes(2, cross, local, set3, energies)
    all_sets = [(set0, amps0), (set1, amps1), (set2, amps2), (set3, amps3)]
    got = {}
    before = {2: density(all_sets[:3], None, 2, F32)}
    for k in (2, 1, 3):
        if k in before:
            part = density(all_sets[3:], before[k], k, BF16)
        else:
            part = density(all_sets, None, k, BF16)
        got[k] = send(part, ALONG[RING - k])
    mine = density(all_sets, None, 0, F32)
    out = finish(mine, [got[k] for k in (1, 2, 3)])
    return out.reshape(ROWS, 2, 2, TILE).transpose(0, 2, 1, 3).reshape(ROWS, 2, 2 * TILE)


def solution(mesh):
    return jax.shard_map(
        steps,
        mesh=mesh,
        in_specs=(P("aux", "occ", "virt"), P(), P()),
        out_specs=P("aux", "occ", "virt"),
        check_vma=False,
    )
```

```python
import functools

import jax
import jax.numpy as jnp
from jax import lax
from jax.experimental import pallas as pl
from jax.experimental.pallas import tpu as pltpu
from jax.sharding import PartitionSpec as P


AXES = ("occ", "virt", "aux")
HIGH, LONG, LOW, CORES, RING = 2, 4, 2, 2, 4
BLOCKS = HIGH * LONG
ROWS, TILE = 768, 128
F32, BF16 = jnp.float32, jnp.bfloat16
LIMIT = 6 << 20


def moves(place):
    pairs = []
    for z_hi in range(HIGH):
        for y in range(LONG):
            for z_lo in range(LOW):
                for core in range(CORES):
                    for x in range(RING):
                        ends = []
                        for h, w, l, c, r in ((z_hi, y, z_lo, core, x), place(z_hi, y, z_lo, core, x)):
                            ends.append((((h * LONG + w) * LOW + l) * CORES + c) * RING + r)
                        pairs.append(tuple(ends))
    return pairs


def chain_step(z_hi, y, z_lo, core, x):
    if y < LONG - 1:
        return z_hi, y + 1, z_lo, core, x
    return 1 - z_hi, 0, 1 - z_lo, core, x


def back_step(z_hi, y, z_lo, core, x):
    if y == 2:
        return 1 - z_hi, 1, 1 - z_lo, core, x
    return z_hi, (y - 1) % LONG, z_lo, core, x


NEXT = moves(chain_step)
PREV = moves(back_step)
PAIR = moves(lambda h, y, l, c, x: (h, y, 1 - l, c, x))
CORE = moves(lambda h, y, l, c, x: (h, y, l, 1 - c, x))
ALONG = [moves(lambda h, y, l, c, x, k=k: (h, y, l, c, (x + k) % RING)) for k in range(RING)]


def send(value, pairs):
    return lax.ppermute(value, AXES, pairs)


def prepare_body(factors_ref, turned_ref, *refs):
    firsts, rests, wide = refs[:3], refs[3:6], refs[6]
    x = lax.axis_index("aux")
    wide[...] = factors_ref[...].astype(F32)
    for q in range(RING):
        value = wide[pl.ds(2 * (q % 2) + q // 2, ROWS, stride=RING), :].astype(BF16)
        t = lax.rem(q - x + RING, RING)
        turned_ref[t] = value
        for k in (1, 2, 3):

            @pl.when(t == k)
            def _():
                firsts[k - 1][...] = value

            @pl.when(t != k)
            def _():
                rests[k - 1][lax.rem(t - k - 1 + 2 * RING, RING)] = value


def prepare(factors):
    rows = factors.reshape(ROWS, 2, 2, TILE).transpose(0, 2, 1, 3).reshape(RING * ROWS, TILE)
    return pl.pallas_call(
        prepare_body,
        out_shape=[pltpu.VMEM((RING, ROWS, TILE), BF16)]
        + [pltpu.VMEM((ROWS, TILE), BF16)] * 3
        + [pltpu.VMEM((3, ROWS, TILE), BF16)] * 3,
        in_specs=[VMEM],
        out_specs=[VMEM] * 7,
        scratch_shapes=[pltpu.VMEM((RING * ROWS, TILE), F32)],
        name="prepare",
        compiler_params=pltpu.CompilerParams(vmem_limit_bytes=LIMIT),
    )(rows)


class Gathered:
    def __init__(self):
        self.arrays = []

    def block(self, array, index):
        for at, known in enumerate(self.arrays):
            if known is array:
                return at, index
        self.arrays.append(array)
        return len(self.arrays) - 1, index

    def piece(self, blocks):
        return [self.block(*block) for block in blocks]


def amplitudes_body(step, labels, local, pieces, *refs):
    occ_ref, lane_ref, out_ref = refs[-3:]
    load = lambda block: refs[block[0]][block[1]]
    part = lax.axis_index("occ")
    virt = lax.axis_index("virt")
    x = lax.axis_index("aux")
    y = lax.rem(part, LONG)
    core = lax.rem(virt, CORES)
    low = lax.rem(lax.div(virt, CORES) + jnp.where(y < step, 1, 0), LOW)
    half = lax.rem(x, 2)
    eo_j = occ_ref[2 * lax.rem(part - step + BLOCKS, BLOCKS) + lax.div(x, 2)]
    lanes = []
    for r in range(RING):
        q = lax.rem(x + r, RING)
        eo_i = occ_ref[2 * part + lax.div(q, 2)]
        lanes.append((eo_i + eo_j) - lane_ref[pl.ds(2 * virt + lax.rem(q, 2), 1), :])
    lane = jnp.concatenate(lanes, axis=1)
    for n in range(0, len(labels), 2):
        total = None
        for k in range(RING):
            wide = jnp.concatenate([load(pieces[n][k]), load(pieces[n + 1][k])], axis=1)
            mine = jnp.concatenate([load(local[r][k]) for r in range(RING)], axis=1)
            given = lax.dot_general(wide, mine, (((0,), (0,)), ((), ())), preferred_element_type=F32)
            total = given if total is None else total + given
        for m in (0, 1):
            other_low, other_core = labels[n + m]
            l = lax.rem(low + other_low, LOW)
            c = lax.rem(core + other_core, CORES)
            ev_b = lane_ref[pl.ds(2 * (CORES * l + c) + half, 1), :]
            column = jnp.transpose(jnp.broadcast_to(ev_b, (TILE, TILE)))
            gap = lane - jnp.concatenate([column] * RING, axis=1)
            ints = total[TILE * m : TILE * m + TILE, :]
            out_ref[TILE * (n + m) : TILE * (n + m) + TILE, :] = (ints / gap).astype(BF16)


VMEM = pl.BlockSpec(memory_space=pltpu.VMEM)


def here(values):
    return [pltpu.with_memory_space_constraint(value, pltpu.VMEM) for value in values]


def amplitudes(step, labels, local, pieces, energies):
    gathered = Gathered()
    local = [gathered.piece(blocks) for blocks in local]
    pieces = [gathered.piece(blocks) for blocks in pieces]
    return pl.pallas_call(
        functools.partial(amplitudes_body, step, labels, local, pieces),
        out_shape=pltpu.VMEM((TILE * len(labels), RING * TILE), BF16),
        in_specs=[VMEM] * len(gathered.arrays) + [pl.BlockSpec(memory_space=pltpu.SMEM), VMEM],
        out_specs=VMEM,
        compiler_params=pltpu.CompilerParams(vmem_limit_bytes=LIMIT),
    )(*here(gathered.arrays), *energies)


def density_body(groups, before, chunk, *refs):
    out_ref = refs[-1]
    deep = 256

    def step(k, rows):
        total = None
        for pieces, amps in groups:
            wide = jnp.concatenate([refs[piece[k][0]][piece[k][1], rows, :] for piece in pieces], axis=1)
            given = jnp.dot(wide, refs[amps][...], preferred_element_type=F32)
            total = given if total is None else total + given
        if before is not None:
            total = total + (refs[before][k, rows, :] if chunk is None else refs[before][rows, :])
        return total.astype(out_ref.dtype)

    for i in range(ROWS // deep):
        rows = slice(deep * i, deep * i + deep)
        if chunk is None:
            for k in range(RING):
                out_ref[k, rows, :] = step(k, rows)
        else:
            out_ref[rows, :] = step(chunk, rows)


def density(groups, before, chunk, kind):
    gathered = Gathered()
    places = []
    for pieces, amps in groups:
        if chunk is not None:
            pieces = [[piece[chunk]] * RING for piece in pieces]
        places.append(([gathered.piece(piece) for piece in pieces], gathered.block(amps, 0)[0]))
    held = None if before is None else gathered.block(before, 0)[0]
    shape = (RING, ROWS, RING * TILE) if chunk is None else (ROWS, RING * TILE)
    return pl.pallas_call(
        functools.partial(density_body, places, held, chunk),
        out_shape=pltpu.VMEM(shape, kind),
        in_specs=[VMEM] * len(gathered.arrays),
        out_specs=VMEM,
        compiler_params=pltpu.CompilerParams(vmem_limit_bytes=LIMIT),
    )(*here(gathered.arrays))


def finish_body(own_ref, *refs):
    got, out_ref = refs[:-1], refs[-1]
    x = lax.axis_index("aux")
    columns = []
    for r in range(RING):
        total = own_ref[:, TILE * r : TILE * r + TILE]
        for k in (1, 3):
            q = (r - k) % RING
            total = total + got[k // 2][:, TILE * q : TILE * q + TILE].astype(F32)
        columns.append(total)
    for v in range(RING):

        @pl.when(x == v)
        def _():
            for q in range(RING):
                at = 2 * (q % 2) + q // 2
                out_ref[pl.ds(at, ROWS, stride=RING), :] = columns[(q - v) % RING]


def middle_body(own_ref, got_ref, out_ref):
    for r in range(RING):
        q = (r - 2) % RING
        got = got_ref[:, TILE * q : TILE * q + TILE].astype(F32)
        out_ref[:, TILE * r : TILE * r + TILE] = own_ref[:, TILE * r : TILE * r + TILE] + got


def middle(own, got):
    return pl.pallas_call(
        middle_body,
        out_shape=pltpu.VMEM((ROWS, RING * TILE), F32),
        in_specs=[VMEM] * 2,
        out_specs=VMEM,
        name="middle",
        compiler_params=pltpu.CompilerParams(vmem_limit_bytes=LIMIT),
    )(*here([own, got]))


def finish(own, got):
    return pl.pallas_call(
        finish_body,
        out_shape=jax.ShapeDtypeStruct((RING * ROWS, TILE), F32),
        in_specs=[VMEM] * 3,
        out_specs=VMEM,
        name="finish",
        compiler_params=pltpu.CompilerParams(vmem_limit_bytes=LIMIT),
    )(*here([own, *got]))


def steps(factors, occ_energy, virt_energy):
    energies = (occ_energy, virt_energy.reshape(8, TILE))

    turned, *ready = prepare(factors)
    came = {k: send(ready[k - 1], ALONG[k]) for k in (1, 2, 3)}
    rest = {k: send(ready[k + 2], ALONG[k]) for k in (1, 2, 3)}
    own = (jnp.stack([turned[0], came[1]]), jnp.stack([came[2], came[3]]))

    both = (0, 1)
    y1 = [send(own[h], NEXT) for h in both]
    z0 = [send(own[h], PAIR) for h in both]
    m1 = [send(own[h], PREV) for h in both]
    m2 = [send(m1[h], PREV) for h in both]
    u1 = send(z0[0], NEXT)
    z1 = send(y1[1], PAIR)
    z2 = send(m2[0], PAIR)
    u2 = send(z1, NEXT)
    swap = lambda pair: [send(pair[h], CORE) for h in both]
    own_c = swap(own)
    z0_c = swap(z0)
    y1_c = swap(y1)
    far_c = swap((u1, z1))
    m2_c = swap(m2)
    last_c = swap((z2, u2))

    halves = lambda low, high: [(low, 0), (low, 1), (high, 0), (high, 1)]
    local = [halves(*own)]
    for r in (1, 2, 3):
        local.append([(turned, r)] + [(rest[k], r - 1) for k in (1, 2, 3)])

    same = [(0, 0), (0, 1)]
    cross = [(1, 0), (1, 1)]
    set0 = [halves(*own), halves(*own_c), halves(*z0), halves(*z0_c)]
    set1 = [halves(*y1), halves(*y1_c), halves(u1, z1), halves(*far_c)]
    set2 = [halves(*m2), halves(*m2_c)]
    set3 = [halves(z2, u2), halves(*last_c)]
    amps0 = amplitudes(0, same + cross, local, set0, energies)
    amps1 = amplitudes(1, same + cross, local, set1, energies)
    amps2 = amplitudes(2, same, local, set2, energies)
    amps3 = amplitudes(2, cross, local, set3, energies)
    all_sets = [(set0, amps0), (set1, amps1), (set2, amps2), (set3, amps3)]
    got = {}
    before = {2: density(all_sets[:3], None, 2, F32)}
    for k in (2, 1, 3):
        if k in before:
            part = density(all_sets[3:], before[k], k, BF16)
        else:
            part = density(all_sets, None, k, BF16)
        got[k] = send(part, ALONG[RING - k])
    mine = density(all_sets, None, 0, F32)
    out = finish(middle(mine, got[2]), [got[1], got[3]])
    return out.reshape(ROWS, 2, 2, TILE).transpose(0, 2, 1, 3).reshape(ROWS, 2, 2 * TILE)


def solution(mesh):
    return jax.shard_map(
        steps,
        mesh=mesh,
        in_specs=(P("aux", "occ", "virt"), P(), P()),
        out_specs=P("aux", "occ", "virt"),
        check_vma=False,
    )
```
